512 devices in a mesh: blk: 64 (over y, z_hi, core), req: 8 (over z_lo, x).
Axes of the slice: x: 4, y: 8, z: 8 (z_hi: 4, z_lo: 2; z = z_hi * 2 + z_lo), core: 2. Of those that a mesh axis runs over, the one named last changes fastest.
Arguments:
- tokens: bfloat16 [8192, 1024], P('blk'), may hold values from -6 to 6
- w_qkv: bfloat16 [1024, 3, 1024], P(None, None, 'req'), may hold values from -0.1875 to 0.1875
- w_out: bfloat16 [1024, 1024], P('req'), may hold values from -0.75 to 0.75
- k_pages: bfloat16 [1280, 128, 1024], P('blk', None, 'req'), may hold values from -512 to 512
- v_pages: bfloat16 [1280, 128, 1024], P('blk', None, 'req'), may hold values from -18 to 18
- page_table: int32 [320, 4], P('blk'), may hold values from 0 to 19, as said below
- cache_lens: int32 [320], P('blk'), may hold values from 1 to 512, as said below
- norm1_gain: float32 [1024], replicated, may hold values from 0.5 to 1.5
- norm1_shift: float32 [1024], replicated, may hold values from -3 to 3
- w_up: bfloat16 [1024, 4096], P(None, 'blk'), may hold values from -0.1875 to 0.1875
- w_down: bfloat16 [4096, 1024], P('blk'), may hold values from -0.1875 to 0.1875
- norm2_gain: float32 [1024], replicated, may hold values from 0.5 to 1.5
- norm2_shift: float32 [1024], replicated, may hold values from -3 to 3
Outputs:
- layer_out: bfloat16 [8192, 1024], P(('blk', 'req'))
The draws below stay inside these ranges and needn't reach their ends.
Inputs may be any that keep to these rules, and one draw needn't show every extreme that they name: `page_table`: the 5 rows of one request group name every page of that group's pool exactly once. `cache_lens`: every request group has at least one request whose cache is full.
All inputs are finite; a program needn't handle non-finite values.
Results may differ from the reference program's by a relative error of at most 0.02.
Values may be sent and summed in bfloat16 or wider, within the bound.
A program may use at most 64 MiB of HBM per device.

```python
import jax
import jax.numpy as jnp
from jax import lax

D = 1024
HEADS = 16
FF = 4096
HD = 64
DEC = 4
PAGE = 128
MAXP = 4
TOK_DEV = 128
TOKENS = 8192
PAGES_DEV = 20
REQS = 320
N_BLK = 64


def draw_page_table(key, part):
    key_list = jax.random.split(key, N_BLK)
    orders = jax.vmap(lambda single_key: jax.random.permutation(single_key, PAGES_DEV))(key_list)
    return orders.reshape(N_BLK * (DEC + 1), MAXP).astype(jnp.int32)


def draw_cache_lens(key, part):
    key_one, key_two, key_three = jax.random.split(key, 3)
    longest = MAXP * PAGE
    drawn_lens = jax.random.randint(key_one, (N_BLK, DEC + 1), 1, longest + 1)
    full_col = jax.random.randint(key_two, (N_BLK, 1), 0, DEC + 1)
    column_ids = jnp.arange(DEC + 1)[None, :]
    drawn_lens = jnp.where(column_ids == full_col, longest, drawn_lens)
    short_blk = jax.random.randint(key_three, (), 0, N_BLK)
    short_col = (full_col[short_blk, 0] + 1) % (DEC + 1)
    row_ids = jnp.arange(N_BLK)[:, None]
    drawn_lens = jnp.where((row_ids == short_blk) & (column_ids == short_col), 1, drawn_lens)
    return drawn_lens.reshape(N_BLK * (DEC + 1)).astype(jnp.int32)


def draw_k_pages(key, part):
    key_one = jax.random.fold_in(jax.random.fold_in(key, 11), 0)
    shape_all = (N_BLK * PAGES_DEV, PAGE, HEADS * HD)
    values = jnp.clip(jax.random.normal(key_one, shape_all, jnp.float32), -6.0, 6.0)
    return values.astype(jnp.bfloat16)


def steps_of(own_key, shape, cuts, smallest, top_value):
    factor_of, own = 1.0, jax.random.fold_in(own_key, 6)
    for position, shards_of in cuts:
        heights = jnp.exp(jax.random.uniform(jax.random.fold_in(own, position), (shards_of,), jnp.float32, smallest / len(cuts), top_value / len(cuts)))
        factor_of = factor_of * jnp.repeat(heights, shape[position] // shards_of).reshape([-1 if axis == position else 1 for axis in range(len(shape))])
    return factor_of


def noise(own_key, shape, deviation, reach, shards=(), held_as=jnp.bfloat16):
    drawn = jax.random.normal(own_key, shape, jnp.float32) * deviation
    if len(shards) > 0:
        drawn = steps_of(own_key, shape, shards, -0.22, 0.18) * drawn
    return jnp.clip(drawn, min=-reach, max=reach).astype(held_as)


def setup_inputs(seed: int = 0) -> dict:
    streams_of = jax.random.split(jax.random.key(seed), 14)
    return {
        "tokens": noise(streams_of[0], (TOKENS, D), 1.0, 6.0, ((0, 64),)),
        "w_qkv": noise(streams_of[1], (D, 3, HEADS * HD), D ** -0.5, 0.1875, ((2, 8),)),
        "w_out": noise(streams_of[2], (HEADS * HD, D), HD ** -0.5, 0.75, ((0, 8),)),
        "k_pages": draw_k_pages(jax.random.fold_in(streams_of[13], 71), 0),
        "v_pages": noise(streams_of[4], (REQS * MAXP, PAGE, HEADS * HD), 3.0, 18.0, ((0, 64), (2, 8))),
        "page_table": draw_page_table(jax.random.fold_in(streams_of[13], 71), 0),
        "cache_lens": draw_cache_lens(jax.random.fold_in(streams_of[13], 71), 0),
        "norm1_gain": jnp.clip(1.0 + 0.1 * jax.random.normal(streams_of[7], (D,), jnp.float32), 0.5, 1.5),
        "norm1_shift": noise(streams_of[8], (D,), 0.5, 3.0, (), jnp.float32),
        "w_up": noise(streams_of[9], (D, FF), D ** -0.5, 0.1875, ((1, 64),)),
        "w_down": noise(streams_of[10], (FF, D), (FF // 4) ** -0.5, 0.1875, ((0, 64),)),
        "norm2_gain": jnp.clip(1.0 + 0.1 * jax.random.normal(streams_of[11], (D,), jnp.float32), 0.5, 1.5),
        "norm2_shift": noise(streams_of[12], (D,), 0.5, 3.0, (), jnp.float32),
    }


epsilon = 1e-05
masked_score = -1e+30

def widened(values):
    return lax.optimization_barrier(values).astype(jnp.float32)

def rounded(values):
    return widened(values.astype(jnp.bfloat16))

def layer_norm(values, gain_vec, shift_vec):
    center = values - lax.optimization_barrier(jnp.mean(values, axis=-1, keepdims=True))
    spread = lax.optimization_barrier(jnp.mean(center * center, axis=-1, keepdims=True))
    return center * lax.rsqrt(spread + epsilon) * gain_vec + shift_vec

def attend(queries, key_new, value_new, key_pool, value_pool, page_map, lengths):
    requests = page_map.shape[0]
    stretch_len = queries.shape[0] - (requests - 1)
    head_count = key_pool.shape[2]
    head_size = key_pool.shape[3]
    key_seq = widened(key_pool[page_map].reshape(requests, -1, head_count, head_size))
    value_seq = widened(value_pool[page_map].reshape(requests, -1, head_count, head_size))
    queries = widened(queries)
    key_new = widened(key_new)
    value_new = widened(value_new)
    scale_factor = head_size ** (-0.5)
    key_span = key_seq.shape[1]
    positions = jnp.arange(key_span)
    prompt_query = queries[:stretch_len]
    cache_scores = jnp.einsum('chd,shd->hcs', prompt_query, key_seq[0]) * scale_factor
    cache_scores = jnp.where(positions[None, None, :] < lengths[0], cache_scores, masked_score)
    stretch_scores = jnp.einsum('chd,jhd->hcj', prompt_query, key_new[:stretch_len]) * scale_factor
    causal = jnp.arange(stretch_len)[:, None] >= jnp.arange(stretch_len)[None, :]
    stretch_scores = jnp.where(causal[None], stretch_scores, masked_score)
    top_score = jnp.maximum(lax.optimization_barrier(jnp.max(cache_scores, -1, keepdims=True)), lax.optimization_barrier(jnp.max(stretch_scores, -1, keepdims=True)))
    cache_exp = jnp.exp(cache_scores - top_score)
    stretch_exp = jnp.exp(stretch_scores - top_score)
    exp_total = lax.optimization_barrier(jnp.sum(cache_exp, -1, keepdims=True)) + lax.optimization_barrier(jnp.sum(stretch_exp, -1, keepdims=True))
    cache_weight = rounded(cache_exp / exp_total)
    stretch_weight = rounded(stretch_exp / exp_total)
    prompt_out = jnp.einsum('hcs,shd->chd', cache_weight, value_seq[0]) + jnp.einsum('hcj,jhd->chd', stretch_weight, value_new[:stretch_len])
    step_query = queries[stretch_len:]
    step_scores = jnp.einsum('rhd,rshd->rhs', step_query, key_seq[1:]) * scale_factor
    step_scores = jnp.where(positions[None, None, :] < lengths[1:, None, None], step_scores, masked_score)
    self_score = lax.optimization_barrier(jnp.sum(step_query * key_new[stretch_len:], axis=-1))[..., None] * scale_factor
    step_top = jnp.maximum(lax.optimization_barrier(jnp.max(step_scores, -1, keepdims=True)), self_score)
    step_exp = jnp.exp(step_scores - step_top)
    self_exp = jnp.exp(self_score - step_top)
    step_total = lax.optimization_barrier(jnp.sum(step_exp, -1, keepdims=True)) + self_exp
    step_weight = rounded(step_exp / step_total)
    self_weight = rounded(self_exp / step_total)
    step_out = jnp.einsum('rhs,rshd->rhd', step_weight, value_seq[1:]) + self_weight * value_new[stretch_len:]
    merged = jnp.concatenate([prompt_out, step_out], axis=0)
    return merged.astype(jnp.bfloat16).reshape(queries.shape[0], head_count * head_size)

def reference(tokens, w_qkv, w_out, k_pages, v_pages, page_table, cache_lens, norm1_gain, norm1_shift, w_up, w_down, norm2_gain, norm2_shift):
    projected = jnp.dot(tokens, w_qkv.reshape(D, 3 * HEADS * HD), preferred_element_type=jnp.float32).astype(jnp.bfloat16)
    projected = projected.reshape(N_BLK, TOK_DEV, 3, HEADS, HD)
    key_pools = k_pages.reshape(N_BLK, PAGES_DEV, PAGE, HEADS, HD)
    value_pools = v_pages.reshape(N_BLK, PAGES_DEV, PAGE, HEADS, HD)
    tables = page_table.reshape(N_BLK, DEC + 1, MAXP)
    lengths = cache_lens.reshape(N_BLK, DEC + 1)

    def per_group(inputs):
        group_proj, key_pool, value_pool, page_map, group_lens = inputs
        return attend(group_proj[:, 0], group_proj[:, 1], group_proj[:, 2], key_pool, value_pool, page_map, group_lens)
    attended = lax.map(per_group, (projected, key_pools, value_pools, tables, lengths)).reshape(TOKENS, HEADS * HD)
    head_mixed = jnp.dot(attended, w_out, preferred_element_type=jnp.float32)
    normed = layer_norm(widened(tokens) + head_mixed, norm1_gain, norm1_shift).astype(jnp.bfloat16)
    hidden = jax.nn.gelu(jnp.dot(normed, w_up, preferred_element_type=jnp.float32), approximate=False).astype(jnp.bfloat16)
    branch = jnp.dot(hidden, w_down, preferred_element_type=jnp.float32)
    return layer_norm(widened(normed) + branch, norm2_gain, norm2_shift).astype(jnp.bfloat16)
```

```python
import jax
import jax.numpy as jnp
from jax import lax
from jax.experimental import pallas as pl
from jax.experimental.pallas import tpu as pltpu
from jax.sharding import PartitionSpec as P

HD = 64
MESH = pl.DeviceIdType.MESH
epsilon = 1e-05
masked_score = -1e30
NT = (((1,), (1,)), ((), ()))


def layer_norm(values, gain_vec, shift_vec):
    center = values - jnp.mean(values, axis=-1, keepdims=True)
    spread = jnp.mean(center * center, axis=-1, keepdims=True)
    return center * lax.rsqrt(spread + epsilon) * gain_vec + shift_vec


def attend(queries, key_new, value_new, key_pool, value_pool, page_map, lengths):
    requests = page_map.shape[0]
    stretch_len = queries.shape[0] - (requests - 1)
    head_count = key_pool.shape[2]
    head_size = key_pool.shape[3]
    key_seq = key_pool[page_map].reshape(requests, -1, head_count, head_size)
    value_seq = value_pool[page_map].reshape(requests, -1, head_count, head_size)
    scale_factor = head_size ** (-0.5)
    key_span = key_seq.shape[1]
    positions = jnp.arange(key_span)
    prompt_query = queries[:stretch_len]
    cache_scores = (
        jnp.einsum("chd,shd->hcs", prompt_query, key_seq[0], preferred_element_type=jnp.float32)
        * scale_factor
    )
    cache_scores = jnp.where(positions[None, None, :] < lengths[0], cache_scores, masked_score)
    stretch_scores = (
        jnp.einsum(
            "chd,jhd->hcj", prompt_query, key_new[:stretch_len], preferred_element_type=jnp.float32
        )
        * scale_factor
    )
    causal = jnp.arange(stretch_len)[:, None] >= jnp.arange(stretch_len)[None, :]
    stretch_scores = jnp.where(causal[None], stretch_scores, masked_score)
    top_score = jnp.maximum(
        jnp.max(cache_scores, -1, keepdims=True), jnp.max(stretch_scores, -1, keepdims=True)
    )
    cache_exp = jnp.exp(cache_scores - top_score)
    stretch_exp = jnp.exp(stretch_scores - top_score)
    exp_total = jnp.sum(cache_exp, -1, keepdims=True) + jnp.sum(stretch_exp, -1, keepdims=True)
    cache_weight = (cache_exp / exp_total).astype(jnp.bfloat16)
    stretch_weight = (stretch_exp / exp_total).astype(jnp.bfloat16)
    prompt_out = jnp.einsum(
        "hcs,shd->chd", cache_weight, value_seq[0], preferred_element_type=jnp.float32
    )
    prompt_out = prompt_out + jnp.einsum(
        "hcj,jhd->chd", stretch_weight, value_new[:stretch_len], preferred_element_type=jnp.float32
    )
    step_query = queries[stretch_len:]
    step_scores = (
        jnp.einsum("rhd,rshd->rhs", step_query, key_seq[1:], preferred_element_type=jnp.float32)
        * scale_factor
    )
    step_scores = jnp.where(
        positions[None, None, :] < lengths[1:, None, None], step_scores, masked_score
    )
    self_score = (
        jnp.einsum(
            "rhd,rhd->rh", step_query, key_new[stretch_len:], preferred_element_type=jnp.float32
        )[..., None]
        * scale_factor
    )
    step_top = jnp.maximum(jnp.max(step_scores, -1, keepdims=True), self_score)
    step_exp = jnp.exp(step_scores - step_top)
    self_exp = jnp.exp(self_score - step_top)
    step_total = jnp.sum(step_exp, -1, keepdims=True) + self_exp
    step_weight = (step_exp / step_total).astype(jnp.bfloat16)
    self_weight = (self_exp / step_total).astype(jnp.bfloat16)
    step_out = jnp.einsum(
        "rhs,rshd->rhd", step_weight, value_seq[1:], preferred_element_type=jnp.float32
    )
    step_out = step_out + self_weight.astype(jnp.float32) * value_new[stretch_len:].astype(
        jnp.float32
    )
    merged = jnp.concatenate([prompt_out, step_out], axis=0)
    return merged.astype(jnp.bfloat16).reshape(queries.shape[0], head_count * head_size)


def tail_kernel(
    part_ref,
    tok_ref,
    g1_ref,
    s1_ref,
    pair_ref,
    g2_ref,
    s2_ref,
    out_ref,
    wts,
    head_in,
    rows_in,
    back_out,
    back_in,
    local_sem,
    o_send,
    o_recv,
    i_send,
    i_recv,
    c_send,
    c_recv,
    h_send,
    h_recv,
    y_send,
    y_recv,
    b_send,
    b_recv,
):
    blk = lax.axis_index("blk")
    req = lax.axis_index("req")
    y = blk // 8
    k = (blk // 2) % 4
    core = blk % 2
    zlo = req // 4
    x = req % 4
    step = 2 * zlo - 1
    outer = (y * 8 + ((k + step + 4) % 4) * 2 + core, (1 - zlo) * 4 + x)
    inner = (blk, (1 - zlo) * 4 + x)
    sibling = (blk + 1 - 2 * core, req)

    def across(d):
        return (blk, (req + d) % 8)

    def along(d):
        return (((y + d) % 8) * 8 + blk % 8, req)

    barrier = pltpu.get_barrier_semaphore()
    for peer in [across(d) for d in range(1, 8)] + [along(d) for d in range(1, 8)] + [outer, sibling]:
        pl.semaphore_signal(barrier, inc=1, device_id=peer, device_id_type=MESH)
    pl.semaphore_wait(barrier, 16)

    def copy(src, dst, send, recv, peer):
        return pltpu.make_async_remote_copy(
            src_ref=src,
            dst_ref=dst,
            send_sem=send,
            recv_sem=recv,
            device_id=peer,
            device_id_type=MESH,
        )

    def slot(dk):
        return ((k + dk + 8) % 4) * 2 + core

    from_o = [(zlo, slot(step)), (1 - zlo, slot(step)), (zlo, slot(2 * step))]
    from_i = [(1 - zlo, slot(-step)), (zlo, slot(-step)), (1 - zlo, slot(-2 * step))]
    own = slot(0)

    def at(c):
        return wts.at[c[0], c[1]]

    local = pltpu.make_async_copy(pair_ref, wts.at[:, own], local_sem)
    local.start()
    head = [
        copy(
            part_ref.at[pl.ds(pl.multiple_of(across(d)[1] * 16, 16), 16)],
            head_in.at[d],
            h_send.at[d],
            h_recv.at[d],
            across(d),
        )
        for d in range(1, 8)
    ]
    to_o = [
        copy(pair_ref.at[1 - zlo], wts.at[1 - zlo, own], o_send.at[0], o_recv.at[0], outer),
        copy(pair_ref.at[zlo], wts.at[zlo, own], o_send.at[1], o_recv.at[1], outer),
        copy(at(from_i[0]), at(from_i[0]), o_send.at[2], o_recv.at[2], outer),
    ]
    to_i = [copy(at(c), at(c), i_send.at[j], i_recv.at[j], inner) for j, c in enumerate(from_o)]
    to_c = [
        copy(pair_ref.at[0], wts.at[0, own], c_send.at[0], c_recv.at[0], sibling),
        copy(pair_ref.at[1], wts.at[1, own], c_send.at[1], c_recv.at[1], sibling),
    ] + [
        copy(at(c), at(c), c_send.at[2 + j], c_recv.at[2 + j], sibling)
        for j, c in enumerate(from_o + from_i)
    ]

    for c in head:
        c.start()
    to_o[0].start()
    to_o[1].start()
    to_c[0].start()
    to_c[1].start()

    def relay_o(j):
        to_o[j].wait_recv()
        to_i[j].start()
        to_c[2 + j].start()

    def relay_i(j):
        to_i[j].wait_recv()
        if j == 0:
            to_o[2].start()
        to_c[5 + j].start()

    relay_o(0)
    relay_i(0)

    for c in head:
        c.wait_recv()
    mine = pl.ds(pl.multiple_of(req * 16, 16), 16)
    mixed = part_ref[mine].astype(jnp.float32)
    for d in range(1, 8):
        mixed = mixed + head_in[d].astype(jnp.float32)
    normed = layer_norm(
        tok_ref[mine].astype(jnp.float32) + mixed, g1_ref[...], s1_ref[...]
    ).astype(jnp.bfloat16)
    rows_in[0] = normed
    send_rows = [
        copy(rows_in.at[0], rows_in.at[d], y_send.at[d], y_recv.at[d], along(d))
        for d in (4, 3, 5, 2, 6, 1, 7)
    ]
    for c in send_rows:
        c.start()

    relay_o(1)
    relay_i(1)
    relay_o(2)
    relay_i(2)
    local.wait()
    for c in to_c:
        c.wait_recv()
    for c in send_rows:
        c.wait_recv()

    rows = rows_in[...].reshape(128, 1024)
    up = wts[0].reshape(512, 1024)
    pre = lax.dot_general(rows, up, NT, preferred_element_type=jnp.float32)
    hidden = (0.5 * pre * (1.0 + lax.erf(pre * (2.0**-0.5)))).astype(jnp.bfloat16)
    down = wts[1].reshape(512, 1024)
    total = jnp.dot(hidden, down, preferred_element_type=jnp.float32)
    back_out[...] = total[16:].astype(jnp.bfloat16).reshape(7, 16, 1024)
    send_back = [
        copy(back_out.at[d - 1], back_in.at[d], b_send.at[d], b_recv.at[d], along(8 - d))
        for d in (4, 3, 5, 2, 6, 1, 7)
    ]
    for c in send_back:
        c.start()
    branch = total[:16]
    for c in send_back:
        c.wait_recv()
    for d in range(1, 8):
        branch = branch + back_in[d].astype(jnp.float32)
    out_ref[...] = layer_norm(
        normed.astype(jnp.float32) + branch, g2_ref[...], s2_ref[...]
    ).astype(jnp.bfloat16)
    for c in head + to_o + to_i + to_c + send_rows + send_back:
        c.wait_send()


def tail(partial_out, tokens, norm1_gain, norm1_shift, pair, norm2_gain, norm2_shift):
    dma = pltpu.SemaphoreType.DMA
    return pl.pallas_call(
        tail_kernel,
        out_shape=jax.ShapeDtypeStruct((16, 1024), jnp.bfloat16),
        in_specs=[pl.BlockSpec(memory_space=pltpu.VMEM)] * 7,
        out_specs=pl.BlockSpec(memory_space=pltpu.VMEM),
        scratch_shapes=[
            pltpu.VMEM((2, 8, 64, 1024), jnp.bfloat16),
            pltpu.VMEM((8, 16, 1024), jnp.bfloat16),
            pltpu.VMEM((8, 16, 1024), jnp.bfloat16),
            pltpu.VMEM((7, 16, 1024), jnp.bfloat16),
            pltpu.VMEM((8, 16, 1024), jnp.bfloat16),
            dma,
            dma((3,)),
            dma((3,)),
            dma((3,)),
            dma((3,)),
            dma((8,)),
            dma((8,)),
            dma((8,)),
            dma((8,)),
            dma((8,)),
            dma((8,)),
            dma((8,)),
            dma((8,)),
        ],
        compiler_params=pltpu.CompilerParams(collective_id=0, has_side_effects=True),
    )(
        partial_out,
        tokens,
        norm1_gain.reshape(1, 1024),
        norm1_shift.reshape(1, 1024),
        pair,
        norm2_gain.reshape(1, 1024),
        norm2_shift.reshape(1, 1024),
    )


def on_device(
    tokens,
    w_qkv,
    w_out,
    k_pages,
    v_pages,
    page_table,
    cache_lens,
    norm1_gain,
    norm1_shift,
    w_up,
    w_down,
    norm2_gain,
    norm2_shift,
):
    tok_rows, model_width = tokens.shape
    head_cols = w_qkv.shape[2]
    head_count = head_cols // HD
    pair = jnp.stack([w_up.T, w_down])
    projected = jnp.dot(
        tokens, w_qkv.reshape(model_width, 3 * head_cols), preferred_element_type=jnp.float32
    ).astype(jnp.bfloat16)
    projected = projected.reshape(tok_rows, 3, head_count, HD)
    pool_pages = k_pages.shape[0]
    key_pool = k_pages.reshape(pool_pages, k_pages.shape[1], head_count, HD)
    value_pool = v_pages.reshape(pool_pages, v_pages.shape[1], head_count, HD)
    attended = attend(
        projected[:, 0],
        projected[:, 1],
        projected[:, 2],
        key_pool,
        value_pool,
        page_table,
        cache_lens,
    )
    partial_out = jnp.dot(attended, w_out, preferred_element_type=jnp.float32)
    return tail(
        partial_out.astype(jnp.bfloat16),
        tokens,
        norm1_gain,
        norm1_shift,
        pair,
        norm2_gain,
        norm2_shift,
    )


def solution(mesh):
    return jax.shard_map(
        on_device,
        mesh=mesh,
        in_specs=(
            P("blk", None),
            P(None, None, "req"),
            P("req", None),
            P("blk", None, "req"),
            P("blk", None, "req"),
            P("blk", None),
            P("blk"),
            P(),
            P(),
            P(None, "blk"),
            P("blk", None),
            P(),
            P(),
        ),
        out_specs=P(("blk", "req"), None),
        check_vma=False,
    )
```

```python
import jax
import jax.numpy as jnp
from jax import lax
from jax.experimental import pallas as pl
from jax.experimental.pallas import tpu as pltpu
from jax.sharding import PartitionSpec as P

HD = 64
PROMPT = 124
MESH = pl.DeviceIdType.MESH
epsilon = 1e-05
masked_score = -1e30
NT = (((1,), (1,)), ((), ()))


def layer_norm(values, gain_vec, shift_vec):
    center = values - jnp.mean(values, axis=-1, keepdims=True)
    spread = jnp.mean(center * center, axis=-1, keepdims=True)
    return center * lax.rsqrt(spread + epsilon) * gain_vec + shift_vec


def attention(proj, k_ref, v_ref, table_ref, lens_ref):
    query = (proj[:, :128] * 0.125).astype(jnp.bfloat16)
    key_new = proj[:, 128:256]
    value_new = proj[:, 256:]

    def heads(rows):
        low = lax.broadcasted_iota(jnp.int32, rows.shape, 1) < HD
        zero = jnp.zeros_like(rows)
        return jnp.concatenate([jnp.where(low, rows, zero), jnp.where(low, zero, rows)], axis=0)

    def attend(rows, first, keys, values, valid):
        count = rows.shape[0]
        both = heads(rows)
        old = lax.dot_general(both, keys, NT, preferred_element_type=jnp.float32)
        old = jnp.where(valid, old, masked_score)
        new = lax.dot_general(both, key_new, NT, preferred_element_type=jnp.float32)
        token = lax.broadcasted_iota(jnp.int32, new.shape, 0) % count + first
        other = lax.broadcasted_iota(jnp.int32, new.shape, 1)
        seen = (other == token) | ((other < token) & (token < PROMPT))
        new = jnp.where(seen, new, masked_score)
        top = jnp.maximum(jnp.max(old, -1, keepdims=True), jnp.max(new, -1, keepdims=True))
        old = jnp.exp(old - top)
        new = jnp.exp(new - top)
        total = jnp.sum(old, -1, keepdims=True) + jnp.sum(new, -1, keepdims=True)
        mixed = jnp.dot(old.astype(jnp.bfloat16), values, preferred_element_type=jnp.float32)
        mixed = mixed + jnp.dot(
            new.astype(jnp.bfloat16), value_new, preferred_element_type=jnp.float32
        )
        mixed = mixed / total
        low = lax.broadcasted_iota(jnp.int32, (count, 128), 1) < HD
        return jnp.where(low, mixed[:count], mixed[count:])

    def cached(ref, request):
        return [ref[table_ref[request, p]] for p in range(4)]

    column = lax.broadcasted_iota(jnp.int32, (1, 512), 1)
    prompt = attend(
        query,
        0,
        jnp.concatenate(cached(k_ref, 0), axis=0),
        jnp.concatenate(cached(v_ref, 0), axis=0),
        column < lens_ref[0],
    )
    column = lax.broadcasted_iota(jnp.int32, (32, 2048), 1)
    row = lax.broadcasted_iota(jnp.int32, (32, 2048), 0) % 16 - 12
    valid = jnp.zeros((32, 2048), jnp.bool_)
    for i in range(4):
        position = column - 512 * i
        valid = valid | ((row == i) & (position >= 0) & (position < lens_ref[1 + i]) & (position < 512))
    decode = attend(
        query[112:],
        112,
        jnp.concatenate([page for i in range(4) for page in cached(k_ref, 1 + i)], axis=0),
        jnp.concatenate([page for i in range(4) for page in cached(v_ref, 1 + i)], axis=0),
        valid,
    )
    last = lax.broadcasted_iota(jnp.int32, (16, 128), 0) >= 12
    return jnp.concatenate(
        [prompt[:112], jnp.where(last, decode, prompt[112:])], axis=0
    ).astype(jnp.bfloat16)


def layer_kernel(
    tok_ref,
    wqkv_ref,
    wout_ref,
    k_ref,
    v_ref,
    table_ref,
    lens_ref,
    g1_ref,
    s1_ref,
    pair_ref,
    g2_ref,
    s2_ref,
    out_ref,
    part_ref,
    wts,
    head_in,
    rows_in,
    back_out,
    back_in,
    local_sem,
    o_send,
    o_recv,
    i_send,
    i_recv,
    c_send,
    c_recv,
    h_send,
    h_recv,
    y_send,
    y_recv,
    b_send,
    b_recv,
):
    blk = lax.axis_index("blk")
    req = lax.axis_index("req")
    y = blk // 8
    k = (blk // 2) % 4
    core = blk % 2
    zlo = req // 4
    x = req % 4
    step = 2 * zlo - 1
    outer = (y * 8 + ((k + step + 4) % 4) * 2 + core, (1 - zlo) * 4 + x)
    inner = (blk, (1 - zlo) * 4 + x)
    sibling = (blk + 1 - 2 * core, req)

    def across(d):
        return (blk, (req + d) % 8)

    def along(d):
        return (((y + d) % 8) * 8 + blk % 8, req)

    barrier = pltpu.get_barrier_semaphore()
    for peer in [across(d) for d in range(1, 8)] + [along(d) for d in range(1, 8)] + [outer, sibling]:
        pl.semaphore_signal(barrier, inc=1, device_id=peer, device_id_type=MESH)
    proj = jnp.dot(
        tok_ref[...], wqkv_ref[...], preferred_element_type=jnp.float32
    ).astype(jnp.bfloat16)
    attended = attention(proj, k_ref, v_ref, table_ref, lens_ref)
    part_ref[...] = jnp.dot(
        attended, wout_ref[...], preferred_element_type=jnp.float32
    ).astype(jnp.bfloat16)
    pl.semaphore_wait(barrier, 16)

    def copy(src, dst, send, recv, peer):
        return pltpu.make_async_remote_copy(
            src_ref=src,
            dst_ref=dst,
            send_sem=send,
            recv_sem=recv,
            device_id=peer,
            device_id_type=MESH,
        )

    def slot(dk):
        return ((k + dk + 8) % 4) * 2 + core

    from_o = [(zlo, slot(step)), (1 - zlo, slot(step)), (zlo, slot(2 * step))]
    from_i = [(1 - zlo, slot(-step)), (zlo, slot(-step)), (1 - zlo, slot(-2 * step))]
    own = slot(0)

    def at(c):
        return wts.at[c[0], c[1]]

    local = pltpu.make_async_copy(pair_ref, wts.at[:, own], local_sem)
    local.start()
    head = [
        copy(
            part_ref.at[pl.ds(pl.multiple_of(across(d)[1] * 16, 16), 16)],
            head_in.at[d],
            h_send.at[d],
            h_recv.at[d],
            across(d),
        )
        for d in range(1, 8)
    ]
    to_o = [
        copy(pair_ref.at[1 - zlo], wts.at[1 - zlo, own], o_send.at[0], o_recv.at[0], outer),
        copy(pair_ref.at[zlo], wts.at[zlo, own], o_send.at[1], o_recv.at[1], outer),
        copy(at(from_i[0]), at(from_i[0]), o_send.at[2], o_recv.at[2], outer),
    ]
    to_i = [copy(at(c), at(c), i_send.at[j], i_recv.at[j], inner) for j, c in enumerate(from_o)]
    to_c = [
        copy(pair_ref.at[0], wts.at[0, own], c_send.at[0], c_recv.at[0], sibling),
        copy(pair_ref.at[1], wts.at[1, own], c_send.at[1], c_recv.at[1], sibling),
    ] + [
        copy(at(c), at(c), c_send.at[2 + j], c_recv.at[2 + j], sibling)
        for j, c in enumerate(from_o + from_i)
    ]

    for c in head:
        c.start()
    to_o[0].start()
    to_o[1].start()
    to_c[0].start()
    to_c[1].start()

    def relay_o(j):
        to_o[j].wait_recv()
        to_i[j].start()
        to_c[2 + j].start()

    def relay_i(j):
        to_i[j].wait_recv()
        if j == 0:
            to_o[2].start()
        to_c[5 + j].start()

    relay_o(0)
    relay_i(0)

    for c in head:
        c.wait_recv()
    mine = pl.ds(pl.multiple_of(req * 16, 16), 16)
    mixed = part_ref[mine].astype(jnp.float32)
    for d in range(1, 8):
        mixed = mixed + head_in[d].astype(jnp.float32)
    normed = layer_norm(
        tok_ref[mine].astype(jnp.float32) + mixed, g1_ref[...], s1_ref[...]
    ).astype(jnp.bfloat16)
    rows_in[0] = normed
    send_rows = [
        copy(rows_in.at[0], rows_in.at[d], y_send.at[d], y_recv.at[d], along(d))
        for d in (4, 3, 5, 2, 6, 1, 7)
    ]
    for c in send_rows:
        c.start()

    relay_o(1)
    relay_i(1)
    relay_o(2)
    relay_i(2)
    local.wait()
    for c in to_c:
        c.wait_recv()
    for c in send_rows:
        c.wait_recv()

    rows = rows_in[...].reshape(128, 1024)
    up = wts[0].reshape(512, 1024)
    pre = lax.dot_general(rows, up, NT, preferred_element_type=jnp.float32)
    hidden = (0.5 * pre * (1.0 + lax.erf(pre * (2.0**-0.5)))).astype(jnp.bfloat16)
    down = wts[1].reshape(512, 1024)
    total = jnp.dot(hidden, down, preferred_element_type=jnp.float32)
    back_out[...] = total[16:].astype(jnp.bfloat16).reshape(7, 16, 1024)
    send_back = [
        copy(back_out.at[d - 1], back_in.at[d], b_send.at[d], b_recv.at[d], along(8 - d))
        for d in (4, 3, 5, 2, 6, 1, 7)
    ]
    for c in send_back:
        c.start()
    branch = total[:16]
    for c in send_back:
        c.wait_recv()
    for d in range(1, 8):
        branch = branch + back_in[d].astype(jnp.float32)
    out_ref[...] = layer_norm(
        normed.astype(jnp.float32) + branch, g2_ref[...], s2_ref[...]
    ).astype(jnp.bfloat16)
    for c in head + to_o + to_i + to_c + send_rows + send_back:
        c.wait_send()


def layer(*operands):
    dma = pltpu.SemaphoreType.DMA
    vmem = pl.BlockSpec(memory_space=pltpu.VMEM)
    smem = pl.BlockSpec(memory_space=pltpu.SMEM)
    return pl.pallas_call(
        layer_kernel,
        out_shape=jax.ShapeDtypeStruct((16, 1024), jnp.bfloat16),
        in_specs=[vmem] * 5 + [smem] * 2 + [vmem] * 5,
        out_specs=vmem,
        scratch_shapes=[
            pltpu.VMEM((128, 1024), jnp.bfloat16),
            pltpu.VMEM((2, 8, 64, 1024), jnp.bfloat16),
            pltpu.VMEM((8, 16, 1024), jnp.bfloat16),
            pltpu.VMEM((8, 16, 1024), jnp.bfloat16),
            pltpu.VMEM((7, 16, 1024), jnp.bfloat16),
            pltpu.VMEM((8, 16, 1024), jnp.bfloat16),
            dma,
        ]
        + [dma((3,))] * 4
        + [dma((8,))] * 8,
        compiler_params=pltpu.CompilerParams(
            collective_id=0, has_side_effects=True, vmem_limit_bytes=48 * 2**20
        ),
    )(*operands)


def on_device(
    tokens,
    w_qkv,
    w_out,
    k_pages,
    v_pages,
    page_table,
    cache_lens,
    norm1_gain,
    norm1_shift,
    w_up,
    w_down,
    norm2_gain,
    norm2_shift,
):
    return layer(
        tokens,
        w_qkv.reshape(1024, 384),
        w_out,
        k_pages,
        v_pages,
        page_table,
        cache_lens,
        norm1_gain.reshape(1, 1024),
        norm1_shift.reshape(1, 1024),
        jnp.stack([w_up.T, w_down]),
        norm2_gain.reshape(1, 1024),
        norm2_shift.reshape(1, 1024),
    )


def solution(mesh):
    return jax.shard_map(
        on_device,
        mesh=mesh,
        in_specs=(
            P("blk", None),
            P(None, None, "req"),
            P("req", None),
            P("blk", None, "req"),
            P("blk", None, "req"),
            P("blk", None),
            P("blk"),
            P(),
            P(),
            P(None, "blk"),
            P("blk", None),
            P(),
            P(),
        ),
        out_specs=P(("blk", "req"), None),
        check_vma=False,
    )
```

```python
import jax
import jax.numpy as jnp
from jax import lax
from jax.experimental import pallas as pl
from jax.experimental.pallas import tpu as pltpu
from jax.sharding import PartitionSpec as P

HD = 64
PROMPT = 124
MESH = pl.DeviceIdType.MESH
epsilon = 1e-05
masked_score = -1e30
NT = (((1,), (1,)), ((), ()))


def layer_norm(values, gain_vec, shift_vec):
    center = values - jnp.mean(values, axis=-1, keepdims=True)
    spread = jnp.mean(center * center, axis=-1, keepdims=True)
    return center * lax.rsqrt(spread + epsilon) * gain_vec + shift_vec


def attention(proj, k_ref, v_ref, table_ref, lens_ref):
    query = (proj[:, :128] * 0.125).astype(jnp.bfloat16)
    key_new = proj[:, 128:256]
    value_new = proj[:, 256:]

    def heads(rows):
        low = lax.broadcasted_iota(jnp.int32, rows.shape, 1) < HD
        zero = jnp.zeros_like(rows)
        return jnp.concatenate([jnp.where(low, rows, zero), jnp.where(low, zero, rows)], axis=0)

    def attend(rows, first, keys, values, valid):
        count = rows.shape[0]
        both = heads(rows)
        old = lax.dot_general(both, keys, NT, preferred_element_type=jnp.float32)
        old = jnp.where(valid, old, masked_score)
        new = lax.dot_general(both, key_new, NT, preferred_element_type=jnp.float32)
        token = lax.broadcasted_iota(jnp.int32, new.shape, 0) % count + first
        other = lax.broadcasted_iota(jnp.int32, new.shape, 1)
        seen = (other == token) | ((other < token) & (token < PROMPT))
        new = jnp.where(seen, new, masked_score)
        top = jnp.maximum(jnp.max(old, -1, keepdims=True), jnp.max(new, -1, keepdims=True))
        old = jnp.exp(old - top)
        new = jnp.exp(new - top)
        total = jnp.sum(old, -1, keepdims=True) + jnp.sum(new, -1, keepdims=True)
        mixed = jnp.dot(old.astype(jnp.bfloat16), values, preferred_element_type=jnp.float32)
        mixed = mixed + jnp.dot(
            new.astype(jnp.bfloat16), value_new, preferred_element_type=jnp.float32
        )
        mixed = mixed / total
        low = lax.broadcasted_iota(jnp.int32, (count, 128), 1) < HD
        return jnp.where(low, mixed[:count], mixed[count:])

    def cached(ref, request):
        return [ref[table_ref[p, request]] for p in range(4)]

    column = lax.broadcasted_iota(jnp.int32, (1, 512), 1)
    prompt = attend(
        query,
        0,
        jnp.concatenate(cached(k_ref, 0), axis=0),
        jnp.concatenate(cached(v_ref, 0), axis=0),
        column < lens_ref[0],
    )
    column = lax.broadcasted_iota(jnp.int32, (32, 2048), 1)
    row = lax.broadcasted_iota(jnp.int32, (32, 2048), 0) % 16 - 12
    valid = jnp.zeros((32, 2048), jnp.bool_)
    for i in range(4):
        position = column - 512 * i
        valid = valid | ((row == i) & (position >= 0) & (position < lens_ref[1 + i]) & (position < 512))
    decode = attend(
        query[112:],
        112,
        jnp.concatenate([page for i in range(4) for page in cached(k_ref, 1 + i)], axis=0),
        jnp.concatenate([page for i in range(4) for page in cached(v_ref, 1 + i)], axis=0),
        valid,
    )
    last = lax.broadcasted_iota(jnp.int32, (16, 128), 0) >= 12
    return jnp.concatenate(
        [prompt[:112], jnp.where(last, decode, prompt[112:])], axis=0
    ).astype(jnp.bfloat16)


def layer_kernel(
    tok_ref,
    wqkv_hbm,
    wout_hbm,
    k_hbm,
    v_hbm,
    table_ref,
    lens_ref,
    g1_ref,
    s1_ref,
    up_hbm,
    down_hbm,
    g2_ref,
    s2_ref,
    out_ref,
    wqkv_ref,
    wout_ref,
    k_ref,
    v_ref,
    part_ref,
    wts,
    head_in,
    rows_in,
    back_out,
    back_in,
    local_sem,
    o_send,
    o_recv,
    i_send,
    i_recv,
    c_send,
    c_recv,
    h_send,
    h_recv,
    y_send,
    y_recv,
    b_send,
    b_recv,
):
    blk = lax.axis_index("blk")
    req = lax.axis_index("req")
    y = blk // 8
    k = (blk // 2) % 4
    core = blk % 2
    zlo = req // 4
    x = req % 4
    step = 2 * zlo - 1
    outer = (y * 8 + ((k + step + 4) % 4) * 2 + core, (1 - zlo) * 4 + x)
    inner = (blk, (1 - zlo) * 4 + x)
    sibling = (blk + 1 - 2 * core, req)

    def across(e):
        z = zlo if e < 4 else 1 - zlo
        return (blk, z * 4 + (x + e) % 4)

    def along(d):
        return (((y + d) % 8) * 8 + blk % 8, req)

    def slot(dk):
        return ((k + dk + 8) % 4) * 2 + core

    own = slot(0)
    barrier = pltpu.get_barrier_semaphore()
    for peer in [across(e) for e in range(1, 8)] + [along(d) for d in range(1, 8)] + [outer, sibling]:
        pl.semaphore_signal(barrier, inc=1, device_id=peer, device_id_type=MESH)
    loads = [
        pltpu.make_async_copy(src, dst, local_sem.at[n])
        for n, (src, dst) in enumerate(
            [
                (up_hbm, wts.at[0, own]),
                (down_hbm, wts.at[1, own]),
                (wqkv_hbm, wqkv_ref),
                (k_hbm, k_ref),
                (v_hbm, v_ref),
                (wout_hbm, wout_ref),
            ]
        )
    ]
    for c in loads:
        c.start()

    def copy(src, dst, send, recv, peer):
        return pltpu.make_async_remote_copy(
            src_ref=src,
            dst_ref=dst,
            send_sem=send,
            recv_sem=recv,
            device_id=peer,
            device_id_type=MESH,
        )

    def halves(kind, place):
        return [wts.at[kind, place, pl.ds(32 * h, 32)] for h in range(2)]

    from_o = halves(zlo, slot(step)) + halves(1 - zlo, slot(step)) + halves(zlo, slot(2 * step))
    from_i = halves(1 - zlo, slot(-step)) + halves(zlo, slot(-step)) + halves(1 - zlo, slot(-2 * step))
    mine_o = halves(1 - zlo, own) + halves(zlo, own) + from_i[:2]
    to_o = [copy(c, c, o_send.at[n], o_recv.at[n], outer) for n, c in enumerate(mine_o)]
    to_i = [copy(c, c, i_send.at[n], i_recv.at[n], inner) for n, c in enumerate(from_o)]
    to_c = [
        copy(c, c, c_send.at[n], c_recv.at[n], sibling)
        for n, c in enumerate(from_o + from_i + [wts.at[0, own], wts.at[1, own]])
    ]
    far = (6, 2, 5, 7, 1, 3, 4)
    head = [
        copy(
            part_ref.at[pl.ds(pl.multiple_of(across(e)[1] * 16, 16), 16)],
            head_in.at[e],
            h_send.at[e],
            h_recv.at[e],
            across(e),
        )
        for e in far
    ]

    def relay_o(n):
        to_o[n].wait_recv()
        to_i[n].start()
        to_c[n].start()

    def relay_i(n):
        to_i[n].wait_recv()
        if n < 2:
            to_o[4 + n].start()
        to_c[6 + n].start()

    loads[0].wait()
    loads[1].wait()
    pl.semaphore_wait(barrier, 16)
    for c in to_o[:4] + to_c[12:]:
        c.start()

    loads[2].wait()
    proj = jnp.concatenate(
        [
            jnp.dot(tok_ref[...], wqkv_ref[n], preferred_element_type=jnp.float32).astype(jnp.bfloat16)
            for n in range(3)
        ],
        axis=1,
    )
    loads[3].wait()
    loads[4].wait()
    attended = attention(proj, k_ref, v_ref, table_ref, lens_ref)
    loads[5].wait()
    part_ref[...] = jnp.dot(
        attended, wout_ref[...], preferred_element_type=jnp.float32
    ).astype(jnp.bfloat16)
    for c in head:
        c.start()

    relay_o(0)
    relay_o(1)
    relay_o(2)
    relay_i(0)
    relay_o(3)
    relay_i(1)
    relay_i(2)
    relay_o(4)

    for c in head:
        c.wait_recv()
    mine = pl.ds(pl.multiple_of(req * 16, 16), 16)
    mixed = part_ref[mine].astype(jnp.float32)
    for e in range(1, 8):
        mixed = mixed + head_in[e].astype(jnp.float32)
    normed = layer_norm(
        tok_ref[mine].astype(jnp.float32) + mixed, g1_ref[...], s1_ref[...]
    ).astype(jnp.bfloat16)
    rows_in[0] = normed
    send_rows = {
        d: copy(rows_in.at[0], rows_in.at[d], y_send.at[d], y_recv.at[d], along(d))
        for d in (4, 3, 5, 2, 6, 1, 7)
    }
    for c in send_rows.values():
        c.start()

    relay_i(3)
    relay_o(5)
    relay_i(4)
    relay_i(5)
    for c in to_c:
        c.wait_recv()

    send_back = {}
    for pair in ((4, 0), (3, 5), (2, 6), (1, 7)):
        for d in pair:
            if d:
                send_rows[d].wait_recv()
        rows = jnp.concatenate([rows_in[d] for d in pair], axis=0)
        up = wts[0].reshape(512, 1024)
        pre = lax.dot_general(rows, up, NT, preferred_element_type=jnp.float32)
        hidden = (0.5 * pre * (1.0 + lax.erf(pre * (2.0**-0.5)))).astype(jnp.bfloat16)
        down = wts[1].reshape(512, 1024)
        total = jnp.dot(hidden, down, preferred_element_type=jnp.float32)
        for n, d in enumerate(pair):
            piece = total[16 * n : 16 * n + 16]
            if d == 0:
                branch = piece
            else:
                back_out[d] = piece.astype(jnp.bfloat16)
                send_back[d] = copy(
                    back_out.at[d], back_in.at[d], b_send.at[d], b_recv.at[d], along(8 - d)
                )
                send_back[d].start()
    for d in (4, 3, 5, 2, 6, 1, 7):
        send_back[d].wait_recv()
        branch = branch + back_in[d].astype(jnp.float32)
    out_ref[...] = layer_norm(
        normed.astype(jnp.float32) + branch, g2_ref[...], s2_ref[...]
    ).astype(jnp.bfloat16)
    for c in head + to_o + to_i + to_c + list(send_rows.values()) + list(send_back.values()):
        c.wait_send()


def layer(*operands):
    dma = pltpu.SemaphoreType.DMA
    vmem = pl.BlockSpec(memory_space=pltpu.VMEM)
    smem = pl.BlockSpec(memory_space=pltpu.SMEM)
    hbm = pl.BlockSpec(memory_space=pltpu.HBM)
    half = jnp.bfloat16
    return pl.pallas_call(
        layer_kernel,
        out_shape=jax.ShapeDtypeStruct((16, 1024), half),
        in_specs=[vmem] + [hbm] * 4 + [smem] * 2 + [vmem] * 2 + [hbm] * 2 + [vmem] * 2,
        out_specs=vmem,
        scratch_shapes=[
            pltpu.VMEM((3, 1024, 128), half),
            pltpu.VMEM((128, 1024), half),
            pltpu.VMEM((20, 128, 128), half),
            pltpu.VMEM((20, 128, 128), half),
            pltpu.VMEM((128, 1024), half),
            pltpu.VMEM((2, 8, 64, 1024), half),
            pltpu.VMEM((8, 16, 1024), half),
            pltpu.VMEM((8, 16, 1024), half),
            pltpu.VMEM((8, 16, 1024), half),
            pltpu.VMEM((8, 16, 1024), half),
            dma((6,)),
        ]
        + [dma((6,))] * 4
        + [dma((14,))] * 2
        + [dma((8,))] * 6,
        compiler_params=pltpu.CompilerParams(
            collective_id=0, has_side_effects=True, vmem_limit_bytes=67043328
        ),
    )(*operands)


def on_device(
    tokens,
    w_qkv,
    w_out,
    k_pages,
    v_pages,
    page_table,
    cache_lens,
    norm1_gain,
    norm1_shift,
    w_up,
    w_down,
    norm2_gain,
    norm2_shift,
):
    return layer(
        tokens,
        w_qkv.transpose(1, 0, 2),
        w_out,
        k_pages,
        v_pages,
        page_table.T,
        cache_lens,
        norm1_gain.reshape(1, 1024),
        norm1_shift.reshape(1, 1024),
        w_up.T,
        w_down,
        norm2_gain.reshape(1, 1024),
        norm2_shift.reshape(1, 1024),
    )


def solution(mesh):
    return jax.shard_map(
        on_device,
        mesh=mesh,
        in_specs=(
            P("blk", None),
            P(None, None, "req"),
            P("req", None),
            P("blk", None, "req"),
            P("blk", None, "req"),
            P("blk", None),
            P("blk"),
            P(),
            P(),
            P(None, "blk"),
            P("blk", None),
            P(),
            P(),
        ),
        out_specs=P(("blk", "req"), None),
        check_vma=False,
    )
```

```python
import jax
import jax.numpy as jnp
from jax import lax
from jax.experimental import pallas as pl
from jax.experimental.pallas import tpu as pltpu
from jax.sharding import PartitionSpec as P

HD = 64
PROMPT = 124
MESH = pl.DeviceIdType.MESH
epsilon = 1e-05
masked_score = -1e30
NT = (((1,), (1,)), ((), ()))


def layer_norm(values, gain_vec, shift_vec):
    center = values - jnp.mean(values, axis=-1, keepdims=True)
    spread = jnp.mean(center * center, axis=-1, keepdims=True)
    return center * lax.rsqrt(spread + epsilon) * gain_vec + shift_vec


def attention(proj, k_ref, v_ref, table_ref, lens_ref):
    query = (proj[:, :128] * 0.125).astype(jnp.bfloat16)
    key_new = proj[:, 128:256]
    value_new = proj[:, 256:]

    def heads(rows):
        low = lax.broadcasted_iota(jnp.int32, rows.shape, 1) < HD
        zero = jnp.zeros_like(rows)
        return jnp.concatenate([jnp.where(low, rows, zero), jnp.where(low, zero, rows)], axis=0)

    def attend(rows, first, keys, values, valid):
        count = rows.shape[0]
        both = heads(rows)
        old = lax.dot_general(both, keys, NT, preferred_element_type=jnp.float32)
        old = jnp.where(valid, old, masked_score)
        new = lax.dot_general(both, key_new, NT, preferred_element_type=jnp.float32)
        token = lax.broadcasted_iota(jnp.int32, new.shape, 0) % count + first
        other = lax.broadcasted_iota(jnp.int32, new.shape, 1)
        seen = (other == token) | ((other < token) & (token < PROMPT))
        new = jnp.where(seen, new, masked_score)
        top = jnp.maximum(jnp.max(old, -1, keepdims=True), jnp.max(new, -1, keepdims=True))
        old = jnp.exp(old - top)
        new = jnp.exp(new - top)
        total = jnp.sum(old, -1, keepdims=True) + jnp.sum(new, -1, keepdims=True)
        mixed = jnp.dot(old.astype(jnp.bfloat16), values, preferred_element_type=jnp.float32)
        mixed = mixed + jnp.dot(
            new.astype(jnp.bfloat16), value_new, preferred_element_type=jnp.float32
        )
        mixed = mixed / total
        low = lax.broadcasted_iota(jnp.int32, (count, 128), 1) < HD
        return jnp.where(low, mixed[:count], mixed[count:])

    def cached(ref, request):
        return [ref[table_ref[p, request]] for p in range(4)]

    column = lax.broadcasted_iota(jnp.int32, (1, 512), 1)
    prompt = attend(
        query,
        0,
        jnp.concatenate(cached(k_ref, 0), axis=0),
        jnp.concatenate(cached(v_ref, 0), axis=0),
        column < lens_ref[0],
    )
    column = lax.broadcasted_iota(jnp.int32, (32, 2048), 1)
    row = lax.broadcasted_iota(jnp.int32, (32, 2048), 0) % 16 - 12
    valid = jnp.zeros((32, 2048), jnp.bool_)
    for i in range(4):
        position = column - 512 * i
        valid = valid | ((row == i) & (position >= 0) & (position < lens_ref[1 + i]) & (position < 512))
    decode = attend(
        query[112:],
        112,
        jnp.concatenate([page for i in range(4) for page in cached(k_ref, 1 + i)], axis=0),
        jnp.concatenate([page for i in range(4) for page in cached(v_ref, 1 + i)], axis=0),
        valid,
    )
    last = lax.broadcasted_iota(jnp.int32, (16, 128), 0) >= 12
    return jnp.concatenate(
        [prompt[:112], jnp.where(last, decode, prompt[112:])], axis=0
    ).astype(jnp.bfloat16)


def layer_kernel(
    tok_hbm,
    wqkv_hbm,
    wout_hbm,
    k_hbm,
    v_hbm,
    table_hbm,
    lens_hbm,
    g1_hbm,
    s1_hbm,
    up_hbm,
    down_hbm,
    g2_hbm,
    s2_hbm,
    out_ref,
    tok_ref,
    table_ref,
    lens_ref,
    g1_ref,
    s1_ref,
    g2_ref,
    s2_ref,
    wqkv_ref,
    wout_ref,
    k_ref,
    v_ref,
    part_ref,
    wts,
    head_in,
    rows_in,
    back_out,
    back_in,
    local_sem,
    o_send,
    o_recv,
    i_send,
    i_recv,
    c_send,
    c_recv,
    h_send,
    h_recv,
    y_send,
    y_recv,
    b_send,
    b_recv,
):
    blk = lax.axis_index("blk")
    req = lax.axis_index("req")
    y = blk // 8
    k = (blk // 2) % 4
    core = blk % 2
    zlo = req // 4
    x = req % 4
    step = 2 * zlo - 1
    outer = (y * 8 + ((k + step + 4) % 4) * 2 + core, (1 - zlo) * 4 + x)
    inner = (blk, (1 - zlo) * 4 + x)
    sibling = (blk + 1 - 2 * core, req)

    def across(e):
        z = zlo if e < 4 else 1 - zlo
        return (blk, z * 4 + (x + e) % 4)

    def along(d):
        return (((y + d) % 8) * 8 + blk % 8, req)

    def slot(dk):
        return ((k + dk + 8) % 4) * 2 + core

    own = slot(0)
    barrier = pltpu.get_barrier_semaphore()
    for peer in [across(e) for e in range(1, 8)] + [along(d) for d in range(1, 8)] + [outer, sibling]:
        pl.semaphore_signal(barrier, inc=1, device_id=peer, device_id_type=MESH)
    loads = [
        pltpu.make_async_copy(src, dst, local_sem.at[n])
        for n, (src, dst) in enumerate(
            [
                (up_hbm, wts.at[0, own]),
                (down_hbm, wts.at[1, own]),
                (wqkv_hbm, wqkv_ref),
                (k_hbm, k_ref),
                (v_hbm, v_ref),
                (wout_hbm, wout_ref),
                (tok_hbm, tok_ref),
                (table_hbm, table_ref),
                (lens_hbm, lens_ref),
                (g1_hbm, g1_ref),
                (s1_hbm, s1_ref),
                (g2_hbm, g2_ref),
                (s2_hbm, s2_ref),
            ]
        )
    ]
    for c in loads:
        c.start()

    def copy(src, dst, send, recv, peer):
        return pltpu.make_async_remote_copy(
            src_ref=src,
            dst_ref=dst,
            send_sem=send,
            recv_sem=recv,
            device_id=peer,
            device_id_type=MESH,
        )

    def halves(kind, place):
        return [wts.at[kind, place, pl.ds(16 * h, 16)] for h in range(4)]

    from_o = halves(zlo, slot(step)) + halves(1 - zlo, slot(step)) + halves(zlo, slot(2 * step))
    from_i = halves(1 - zlo, slot(-step)) + halves(zlo, slot(-step)) + halves(1 - zlo, slot(-2 * step))
    mine_o = halves(1 - zlo, own) + halves(zlo, own) + from_i[:4]
    to_o = [copy(c, c, o_send.at[n], o_recv.at[n], outer) for n, c in enumerate(mine_o)]
    to_i = [copy(c, c, i_send.at[n], i_recv.at[n], inner) for n, c in enumerate(from_o)]
    to_c = [
        copy(c, c, c_send.at[n], c_recv.at[n], sibling)
        for n, c in enumerate(from_o + from_i + [wts.at[0, own], wts.at[1, own]])
    ]
    far = (6, 2, 5, 7, 1, 3, 4)
    head = [
        copy(
            part_ref.at[pl.ds(pl.multiple_of(across(e)[1] * 16, 16), 16)],
            head_in.at[e],
            h_send.at[e],
            h_recv.at[e],
            across(e),
        )
        for e in far
    ]

    def relay_o(n):
        to_o[n].wait_recv()
        to_i[n].start()
        to_c[n].start()

    def relay_i(n):
        to_i[n].wait_recv()
        if n < 4:
            to_o[8 + n].start()
        to_c[12 + n].start()

    loads[0].wait()
    loads[1].wait()
    pl.semaphore_wait(barrier, 16)
    for c in to_o[:8] + to_c[24:]:
        c.start()

    loads[2].wait()
    loads[6].wait()
    proj = jnp.concatenate(
        [
            jnp.dot(tok_ref[...], wqkv_ref[n], preferred_element_type=jnp.float32).astype(jnp.bfloat16)
            for n in range(3)
        ],
        axis=1,
    )
    loads[3].wait()
    loads[4].wait()
    loads[7].wait()
    loads[8].wait()
    attended = attention(proj, k_ref, v_ref, table_ref, lens_ref)
    loads[5].wait()
    for c in loads[9:]:
        c.wait()
    part_ref[...] = jnp.dot(
        attended, wout_ref[...], preferred_element_type=jnp.float32
    ).astype(jnp.bfloat16)
    for c in head:
        c.start()

    relay_o(0)
    relay_o(1)
    relay_o(2)
    relay_o(3)
    relay_i(0)
    relay_o(4)
    relay_i(1)
    relay_o(5)
    relay_i(2)
    relay_o(6)
    relay_i(3)
    relay_o(7)
    relay_i(4)
    relay_o(8)
    relay_i(5)
    relay_o(9)

    for c in head:
        c.wait_recv()
    mine = pl.ds(pl.multiple_of(req * 16, 16), 16)
    mixed = part_ref[mine].astype(jnp.float32)
    for e in range(1, 8):
        mixed = mixed + head_in[e].astype(jnp.float32)
    normed = layer_norm(
        tok_ref[mine].astype(jnp.float32) + mixed, g1_ref[...], s1_ref[...]
    ).astype(jnp.bfloat16)
    rows_in[0] = normed
    send_rows = {
        d: copy(rows_in.at[0], rows_in.at[d], y_send.at[d], y_recv.at[d], along(d))
        for d in (4, 3, 5, 2, 6, 1, 7)
    }
    for c in send_rows.values():
        c.start()

    relay_i(6)
    relay_o(10)
    relay_i(7)
    relay_o(11)
    relay_i(8)
    relay_i(9)
    relay_i(10)
    relay_i(11)

    for c in to_c:
        c.wait_recv()

    send_back = {}
    for pair in ((4, 0), (3, 5), (2, 6), (1, 7)):
        for d in pair:
            if d:
                send_rows[d].wait_recv()
        rows = jnp.concatenate([rows_in[d] for d in pair], axis=0)
        up = wts[0].reshape(512, 1024)
        pre = lax.dot_general(rows, up, NT, preferred_element_type=jnp.float32)
        hidden = (0.5 * pre * (1.0 + lax.erf(pre * (2.0**-0.5)))).astype(jnp.bfloat16)
        down = wts[1].reshape(512, 1024)
        total = jnp.dot(hidden, down, preferred_element_type=jnp.float32)
        for n, d in enumerate(pair):
            piece = total[16 * n : 16 * n + 16]
            if d == 0:
                branch = piece
            else:
                back_out[d] = piece.astype(jnp.bfloat16)
                send_back[d] = copy(
                    back_out.at[d], back_in.at[d], b_send.at[d], b_recv.at[d], along(8 - d)
                )
                send_back[d].start()
    for d in (4, 3, 5, 2, 6, 1, 7):
        send_back[d].wait_recv()
        branch = branch + back_in[d].astype(jnp.float32)
    out_ref[...] = layer_norm(
        normed.astype(jnp.float32) + branch, g2_ref[...], s2_ref[...]
    ).astype(jnp.bfloat16)
    for c in head + to_o + to_i + to_c + list(send_rows.values()) + list(send_back.values()):
        c.wait_send()


def layer(*operands):
    dma = pltpu.SemaphoreType.DMA
    vmem = pl.BlockSpec(memory_space=pltpu.VMEM)
    hbm = pl.BlockSpec(memory_space=pltpu.HBM)
    half = jnp.bfloat16
    return pl.pallas_call(
        layer_kernel,
        out_shape=jax.ShapeDtypeStruct((16, 1024), half),
        in_specs=[hbm] * 13,
        out_specs=vmem,
        scratch_shapes=[
            pltpu.VMEM((128, 1024), half),
            pltpu.SMEM((4, 5), jnp.int32),
            pltpu.SMEM((5,), jnp.int32),
        ]
        + [pltpu.VMEM((1, 1024), jnp.float32)] * 4
        + [
            pltpu.VMEM((3, 1024, 128), half),
            pltpu.VMEM((128, 1024), half),
            pltpu.VMEM((20, 128, 128), half),
            pltpu.VMEM((20, 128, 128), half),
            pltpu.VMEM((128, 1024), half),
            pltpu.VMEM((2, 8, 64, 1024), half),
            pltpu.VMEM((8, 16, 1024), half),
            pltpu.VMEM((8, 16, 1024), half),
            pltpu.VMEM((8, 16, 1024), half),
            pltpu.VMEM((8, 16, 1024), half),
            dma((13,)),
        ]
        + [dma((12,))] * 4
        + [dma((26,))] * 2
        + [dma((8,))] * 6,
        compiler_params=pltpu.CompilerParams(
            collective_id=0, has_side_effects=True, vmem_limit_bytes=67043328
        ),
    )(*operands)


def on_device(
    tokens,
    w_qkv,
    w_out,
    k_pages,
    v_pages,
    page_table,
    cache_lens,
    norm1_gain,
    norm1_shift,
    w_up,
    w_down,
    norm2_gain,
    norm2_shift,
):
    return layer(
        tokens,
        w_qkv.transpose(1, 0, 2),
        w_out,
        k_pages,
        v_pages,
        page_table.T,
        cache_lens,
        norm1_gain.reshape(1, 1024),
        norm1_shift.reshape(1, 1024),
        w_up.T,
        w_down,
        norm2_gain.reshape(1, 1024),
        norm2_shift.reshape(1, 1024),
    )


def solution(mesh):
    return jax.shard_map(
        on_device,
        mesh=mesh,
        in_specs=(
            P("blk", None),
            P(None, None, "req"),
            P("req", None),
            P("blk", None, "req"),
            P("blk", None, "req"),
            P("blk", None),
            P("blk"),
            P(),
            P(),
            P(None, "blk"),
            P("blk", None),
            P(),
            P(),
        ),
        out_specs=P(("blk", "req"), None),
        check_vma=False,
    )
```

```python
import jax
import jax.numpy as jnp
from jax import lax
from jax.experimental import pallas as pl
from jax.experimental.pallas import tpu as pltpu
from jax.sharding import PartitionSpec as P

HD = 64
PROMPT = 124
MESH = pl.DeviceIdType.MESH
epsilon = 1e-05
masked_score = -1e30
NT = (((1,), (1,)), ((), ()))


def layer_norm(values, gain_vec, shift_vec):
    center = values - jnp.mean(values, axis=-1, keepdims=True)
    spread = jnp.mean(center * center, axis=-1, keepdims=True)
    return center * lax.rsqrt(spread + epsilon) * gain_vec + shift_vec


def attention(proj, k_ref, v_ref, table_ref, lens_ref):
    query = (proj[:, :128] * 0.125).astype(jnp.bfloat16)
    key_new = proj[:, 128:256]
    value_new = proj[:, 256:]

    def heads(rows):
        low = lax.broadcasted_iota(jnp.int32, rows.shape, 1) < HD
        zero = jnp.zeros_like(rows)
        return jnp.concatenate([jnp.where(low, rows, zero), jnp.where(low, zero, rows)], axis=0)

    def attend(rows, first, keys, values, valid):
        count = rows.shape[0]
        both = heads(rows)
        old = lax.dot_general(both, keys, NT, preferred_element_type=jnp.float32)
        old = jnp.where(valid, old, masked_score)
        new = lax.dot_general(both, key_new, NT, preferred_element_type=jnp.float32)
        token = lax.broadcasted_iota(jnp.int32, new.shape, 0) % count + first
        other = lax.broadcasted_iota(jnp.int32, new.shape, 1)
        seen = (other == token) | ((other < token) & (token < PROMPT))
        new = jnp.where(seen, new, masked_score)
        top = jnp.maximum(jnp.max(old, -1, keepdims=True), jnp.max(new, -1, keepdims=True))
        old = jnp.exp(old - top)
        new = jnp.exp(new - top)
        total = jnp.sum(old, -1, keepdims=True) + jnp.sum(new, -1, keepdims=True)
        mixed = jnp.dot(old.astype(jnp.bfloat16), values, preferred_element_type=jnp.float32)
        mixed = mixed + jnp.dot(
            new.astype(jnp.bfloat16), value_new, preferred_element_type=jnp.float32
        )
        mixed = mixed / total
        low = lax.broadcasted_iota(jnp.int32, (count, 128), 1) < HD
        return jnp.where(low, mixed[:count], mixed[count:])

    def cached(ref, request):
        return [ref[table_ref[p, request]] for p in range(4)]

    column = lax.broadcasted_iota(jnp.int32, (1, 512), 1)
    prompt = attend(
        query,
        0,
        jnp.concatenate(cached(k_ref, 0), axis=0),
        jnp.concatenate(cached(v_ref, 0), axis=0),
        column < lens_ref[0],
    )
    column = lax.broadcasted_iota(jnp.int32, (32, 2048), 1)
    row = lax.broadcasted_iota(jnp.int32, (32, 2048), 0) % 16 - 12
    valid = jnp.zeros((32, 2048), jnp.bool_)
    for i in range(4):
        position = column - 512 * i
        valid = valid | ((row == i) & (position >= 0) & (position < lens_ref[1 + i]) & (position < 512))
    decode = attend(
        query[112:],
        112,
        jnp.concatenate([page for i in range(4) for page in cached(k_ref, 1 + i)], axis=0),
        jnp.concatenate([page for i in range(4) for page in cached(v_ref, 1 + i)], axis=0),
        valid,
    )
    last = lax.broadcasted_iota(jnp.int32, (16, 128), 0) >= 12
    return jnp.concatenate(
        [prompt[:112], jnp.where(last, decode, prompt[112:])], axis=0
    ).astype(jnp.bfloat16)


def layer_kernel(
    tok_hbm,
    wqkv_hbm,
    wout_hbm,
    k_hbm,
    v_hbm,
    table_hbm,
    lens_hbm,
    g1_hbm,
    s1_hbm,
    up_hbm,
    down_hbm,
    g2_hbm,
    s2_hbm,
    out_ref,
    tok_ref,
    table_ref,
    lens_ref,
    g1_ref,
    s1_ref,
    g2_ref,
    s2_ref,
    wqkv_ref,
    wout_ref,
    k_ref,
    v_ref,
    part_ref,
    wts,
    head_in,
    rows_in,
    back_out,
    back_in,
    local_sem,
    o_send,
    o_recv,
    i_send,
    i_recv,
    c_send,
    c_recv,
    h_send,
    h_recv,
    y_send,
    y_recv,
    b_send,
    b_recv,
):
    blk = lax.axis_index("blk")
    req = lax.axis_index("req")
    y = blk // 8
    k = (blk // 2) % 4
    core = blk % 2
    zlo = req // 4
    x = req % 4
    step = 2 * zlo - 1
    outer = (y * 8 + ((k + step + 4) % 4) * 2 + core, (1 - zlo) * 4 + x)
    inner = (blk, (1 - zlo) * 4 + x)
    sibling = (blk + 1 - 2 * core, req)

    def across(e):
        z = zlo if e < 4 else 1 - zlo
        return (blk, z * 4 + (x + e) % 4)

    def along(d):
        return (((y + d) % 8) * 8 + blk % 8, req)

    def slot(dk):
        return ((k + dk + 8) % 4) * 2 + core

    own = slot(0)
    barrier = pltpu.get_barrier_semaphore()
    for peer in [across(e) for e in range(1, 8)] + [along(d) for d in range(1, 8)] + [outer, sibling]:
        pl.semaphore_signal(barrier, inc=1, device_id=peer, device_id_type=MESH)
    loads = [
        pltpu.make_async_copy(src, dst, local_sem.at[n])
        for n, (src, dst) in enumerate(
            [
                (up_hbm, wts.at[0, own]),
                (down_hbm, wts.at[1, own]),
                (wqkv_hbm, wqkv_ref),
                (k_hbm, k_ref),
                (v_hbm, v_ref),
                (wout_hbm, wout_ref),
                (tok_hbm, tok_ref),
                (table_hbm, table_ref),
                (lens_hbm, lens_ref),
                (g1_hbm, g1_ref),
                (s1_hbm, s1_ref),
                (g2_hbm, g2_ref),
                (s2_hbm, s2_ref),
            ]
        )
    ]
    for c in loads:
        c.start()

    def copy(src, dst, send, recv, peer):
        return pltpu.make_async_remote_copy(
            src_ref=src,
            dst_ref=dst,
            send_sem=send,
            recv_sem=recv,
            device_id=peer,
            device_id_type=MESH,
        )

    def halves(kind, place):
        return [wts.at[kind, place, pl.ds(16 * h, 16)] for h in range(4)]

    from_o = halves(zlo, slot(step)) + halves(1 - zlo, slot(step)) + halves(zlo, slot(2 * step))
    from_i = halves(1 - zlo, slot(-step)) + halves(zlo, slot(-step)) + halves(1 - zlo, slot(-2 * step))
    mine_o = halves(1 - zlo, own) + halves(zlo, own) + from_i[:4]
    to_o = [copy(c, c, o_send.at[n], o_recv.at[n], outer) for n, c in enumerate(mine_o)]
    to_i = [copy(c, c, i_send.at[n], i_recv.at[n], inner) for n, c in enumerate(from_o)]
    to_c = [
        copy(c, c, c_send.at[n], c_recv.at[n], sibling)
        for n, c in enumerate(from_o + from_i + [wts.at[0, own], wts.at[1, own]])
    ]
    far = (6, 2, 5, 7, 1, 3, 4)
    head = [
        copy(
            part_ref.at[pl.ds(pl.multiple_of(across(e)[1] * 16, 16), 16)],
            head_in.at[e],
            h_send.at[e],
            h_recv.at[e],
            across(e),
        )
        for e in far
    ]

    def relay_o(n):
        to_o[n].wait_recv()
        to_i[n].start()
        to_c[n].start()

    def relay_i(n):
        to_i[n].wait_recv()
        if n < 4:
            to_o[8 + n].start()
        to_c[12 + n].start()

    loads[0].wait()
    loads[1].wait()
    pl.semaphore_wait(barrier, 16)
    for c in to_o[:8] + to_c[24:]:
        c.start()

    loads[2].wait()
    loads[6].wait()
    proj = jnp.concatenate(
        [
            jnp.dot(tok_ref[...], wqkv_ref[n], preferred_element_type=jnp.float32).astype(jnp.bfloat16)
            for n in range(3)
        ],
        axis=1,
    )
    loads[3].wait()
    loads[4].wait()
    loads[7].wait()
    loads[8].wait()
    attended = attention(proj, k_ref, v_ref, table_ref, lens_ref)
    loads[5].wait()
    for c in loads[9:]:
        c.wait()
    part_ref[...] = jnp.dot(
        attended, wout_ref[...], preferred_element_type=jnp.float32
    ).astype(jnp.bfloat16)
    for c in head:
        c.start()

    relay_o(0)
    relay_o(1)
    relay_o(2)
    relay_o(3)
    relay_i(0)
    relay_o(4)
    relay_i(1)
    relay_o(5)
    relay_i(2)
    relay_o(6)
    relay_i(3)
    relay_o(7)
    relay_i(4)
    relay_o(8)
    relay_i(5)
    relay_o(9)

    for c in head:
        c.wait_recv()
    mine = pl.ds(pl.multiple_of(req * 16, 16), 16)
    mixed = part_ref[mine].astype(jnp.float32)
    for e in range(1, 8):
        mixed = mixed + head_in[e].astype(jnp.float32)
    normed = layer_norm(
        tok_ref[mine].astype(jnp.float32) + mixed, g1_ref[...], s1_ref[...]
    ).astype(jnp.bfloat16)
    rows_in[0] = normed
    send_rows = {
        d: copy(rows_in.at[0], rows_in.at[d], y_send.at[d], y_recv.at[d], along(d))
        for d in (4, 3, 5, 2, 6, 1, 7)
    }
    for c in send_rows.values():
        c.start()

    relay_i(6)
    relay_o(10)
    relay_i(7)
    relay_o(11)
    relay_i(8)
    relay_i(9)
    relay_i(10)
    relay_i(11)

    for c in to_c:
        c.wait_recv()

    send_back = {}
    for pair in ((4, 3, 5, 0), (2, 6, 1, 7)):
        for d in pair:
            if d:
                send_rows[d].wait_recv()
        rows = jnp.concatenate([rows_in[d] for d in pair], axis=0)
        up = wts[0].reshape(512, 1024)
        pre = lax.dot_general(rows, up, NT, preferred_element_type=jnp.float32)
        hidden = (0.5 * pre * (1.0 + lax.erf(pre * (2.0**-0.5)))).astype(jnp.bfloat16)
        down = wts[1].reshape(512, 1024)
        total = jnp.dot(hidden, down, preferred_element_type=jnp.float32)
        for n, d in enumerate(pair):
            piece = total[16 * n : 16 * n + 16]
            if d == 0:
                branch = piece
            else:
                back_out[d] = piece.astype(jnp.bfloat16)
                send_back[d] = copy(
                    back_out.at[d], back_in.at[d], b_send.at[d], b_recv.at[d], along(8 - d)
                )
                send_back[d].start()
    for d in (4, 3, 5, 2, 6, 1, 7):
        send_back[d].wait_recv()
        branch = branch + back_in[d].astype(jnp.float32)
    out_ref[...] = layer_norm(
        normed.astype(jnp.float32) + branch, g2_ref[...], s2_ref[...]
    ).astype(jnp.bfloat16)
    for c in head + to_o + to_i + to_c + list(send_rows.values()) + list(send_back.values()):
        c.wait_send()


def layer(*operands):
    dma = pltpu.SemaphoreType.DMA
    vmem = pl.BlockSpec(memory_space=pltpu.VMEM)
    hbm = pl.BlockSpec(memory_space=pltpu.HBM)
    half = jnp.bfloat16
    return pl.pallas_call(
        layer_kernel,
        out_shape=jax.ShapeDtypeStruct((16, 1024), half),
        in_specs=[hbm] * 13,
        out_specs=vmem,
        scratch_shapes=[
            pltpu.VMEM((128, 1024), half),
            pltpu.SMEM((4, 5), jnp.int32),
            pltpu.SMEM((5,), jnp.int32),
        ]
        + [pltpu.VMEM((1, 1024), jnp.float32)] * 4
        + [
            pltpu.VMEM((3, 1024, 128), half),
            pltpu.VMEM((128, 1024), half),
            pltpu.VMEM((20, 128, 128), half),
            pltpu.VMEM((20, 128, 128), half),
            pltpu.VMEM((128, 1024), half),
            pltpu.VMEM((2, 8, 64, 1024), half),
            pltpu.VMEM((8, 16, 1024), half),
            pltpu.VMEM((8, 16, 1024), half),
            pltpu.VMEM((8, 16, 1024), half),
            pltpu.VMEM((8, 16, 1024), half),
            dma((13,)),
        ]
        + [dma((12,))] * 4
        + [dma((26,))] * 2
        + [dma((8,))] * 6,
        compiler_params=pltpu.CompilerParams(
            collective_id=0, has_side_effects=True, vmem_limit_bytes=67043328
        ),
    )(*operands)


def on_device(
    tokens,
    w_qkv,
    w_out,
    k_pages,
    v_pages,
    page_table,
    cache_lens,
    norm1_gain,
    norm1_shift,
    w_up,
    w_down,
    norm2_gain,
    norm2_shift,
):
    return layer(
        tokens,
        w_qkv.transpose(1, 0, 2),
        w_out,
        k_pages,
        v_pages,
        page_table.T,
        cache_lens,
        norm1_gain.reshape(1, 1024),
        norm1_shift.reshape(1, 1024),
        w_up.T,
        w_down,
        norm2_gain.reshape(1, 1024),
        norm2_shift.reshape(1, 1024),
    )


def solution(mesh):
    return jax.shard_map(
        on_device,
        mesh=mesh,
        in_specs=(
            P("blk", None),
            P(None, None, "req"),
            P("req", None),
            P("blk", None, "req"),
            P("blk", None, "req"),
            P("blk", None),
            P("blk"),
            P(),
            P(),
            P(None, "blk"),
            P("blk", None),
            P(),
            P(),
        ),
        out_specs=P(("blk", "req"), None),
        check_vma=False,
    )
```
